32 devices in a mesh: ctx: 8 (over y, x, core), head: 4 (over z).
Axes of the slice: x: 2, y: 2, z: 4, core: 2. Of those that a mesh axis runs over, the one named last changes fastest.
Arguments:
- hidden_in: bfloat16 [1536, 4096], P('ctx'), may hold values from -10 to 10
- query_soft: bfloat16 [1536, 1024], P('ctx', 'head'), may hold values from -6 to 6
- key_soft: bfloat16 [1536, 512], P('ctx', 'head'), may hold values from -6 to 6
- value_soft: bfloat16 [1536, 512], P('ctx', 'head'), may hold values from -6 to 6
- out_weight: bfloat16 [1024, 4096], P('head'), may hold values from -0.1875 to 0.1875
- query_weight: bfloat16 [4096, 1024], P(None, 'head'), may hold values from -0.09375 to 0.09375
- key_weight: bfloat16 [4096, 1024], P(None, 'head'), may hold values from -0.09375 to 0.09375
- value_weight: bfloat16 [4096, 1024], P(None, 'head'), may hold values from -0.09375 to 0.09375
Outputs:
- linear_out: bfloat16 [1536, 1024], P('ctx', 'head')
The draws below stay inside these ranges and needn't reach their ends.
All inputs are finite; a program needn't handle non-finite values.
Results may differ from the reference program's by a relative error of at most 0.025.
Values may be sent and summed in bfloat16 or wider, within the bound.
No kernel may reach another device: no remote copies, remote signals or barrier semaphores. Data moves between devices by JAX's collectives and lax.ppermute only.
A program may use at most 64 MiB of HBM per device.

```python
import math
import jax
import jax.numpy as jnp
from jax import lax

D = 4096
HEAD_DIM = 128
HEAD_DEV = 2
TOK_DEV = 192
HEADS = 8
KV_HEADS = 4
TOKENS = 1536
N_CTX = 8


def row_scaled(key, row_count, column_count, low_scale, high_scale, clip_at):
    base_key = jax.random.fold_in(key, 1)
    scale_key = jax.random.fold_in(key, 2)
    base = jnp.clip(jax.random.normal(base_key, (row_count, column_count), jnp.float32), -clip_at, clip_at)
    row_scale = jnp.exp(jax.random.uniform(scale_key, (row_count, 1), jnp.float32, math.log(low_scale), math.log(high_scale)))
    return base * row_scale


def draw_hidden_in(key, part):
    rows_part = row_scaled(jax.random.fold_in(key, 11), TOKENS, D, 0.5, 2.0, 4.0)
    column_scale = jnp.exp(jax.random.uniform(jax.random.fold_in(key, 12), (1, D), jnp.float32, math.log(0.3), math.log(3.0)))
    return (0.4 * rows_part * column_scale).astype(jnp.bfloat16)


def drawn_pair(key):
    query_all = row_scaled(jax.random.fold_in(key, 21), TOKENS, HEADS * HEAD_DIM, 0.6, 2.4, 2.5)
    keys_all = row_scaled(jax.random.fold_in(key, 22), TOKENS, KV_HEADS * HEAD_DIM, 0.6, 2.4, 2.5)
    query_all = query_all.reshape(TOKENS, HEADS, HEAD_DIM)
    keys_all = keys_all.reshape(TOKENS, KV_HEADS, HEAD_DIM)
    return (query_all.reshape(TOKENS, HEADS * HEAD_DIM), keys_all.reshape(TOKENS, KV_HEADS * HEAD_DIM))


def draw_query_soft(key, part):
    return drawn_pair(key)[0].astype(jnp.bfloat16)


def draw_key_soft(key, part):
    return drawn_pair(key)[1].astype(jnp.bfloat16)


def levels(stream_key, extent, shards, smallest, largest):
    loudness, own = 1.0, jax.random.fold_in(stream_key, 6)
    for dim, blocks in shards:
        draws = jnp.exp(jax.random.uniform(jax.random.fold_in(own, dim), (blocks,), jnp.float32, smallest / len(shards), largest / len(shards)))
        loudness = loudness * jnp.repeat(draws, extent[dim] // blocks).reshape([-1 if axis == dim else 1 for axis in range(len(extent))])
    return loudness


def bell_draw(stream_key, dims, deviation, limit, pieces=(), kind=jnp.bfloat16):
    array = jax.random.normal(stream_key, dims, jnp.float32) * deviation
    if len(pieces) > 0:
        array = levels(stream_key, dims, pieces, -0.22, 0.18) * array
    return jnp.clip(array, min=-limit, max=limit).astype(kind)


def setup_inputs(seed: int = 0) -> dict:
    seeds = jax.random.split(jax.random.key(seed), 9)
    hidden_in = draw_hidden_in(jax.random.fold_in(seeds[8], 71), 0)
    query_soft = draw_query_soft(jax.random.fold_in(seeds[8], 71), 0)
    key_soft = draw_key_soft(jax.random.fold_in(seeds[8], 71), 0)
    value_soft = bell_draw(seeds[3], (TOKENS, KV_HEADS * HEAD_DIM), 1.0, 6.0, ((0, 8), (1, 4)))
    out_weight = bell_draw(seeds[4], (HEADS * HEAD_DIM, D), (HEADS * HEAD_DIM) ** -0.5, 0.1875, ((0, 4),))
    query_weight = bell_draw(seeds[5], (D, HEADS * HEAD_DIM), D ** -0.5, 0.09375, ((1, 4),))
    key_weight = bell_draw(seeds[6], (D, HEADS * HEAD_DIM), D ** -0.5, 0.09375, ((1, 4),))
    value_weight = bell_draw(seeds[7], (D, HEADS * HEAD_DIM), D ** -0.5, 0.09375, ((1, 4),))
    return dict(hidden_in=hidden_in, query_soft=query_soft, key_soft=key_soft, value_soft=value_soft, out_weight=out_weight, query_weight=query_weight, key_weight=key_weight, value_weight=value_weight)


def rms_rows(values):
    return values * lax.rsqrt(lax.optimization_barrier(jnp.mean(values * values, axis=-1, keepdims=True)) + 1e-06)

def rounded(values):
    return lax.optimization_barrier(values.astype(jnp.bfloat16)).astype(jnp.float32)

def reference(hidden_in, query_soft, key_soft, value_soft, out_weight, query_weight, key_weight, value_weight):
    float_type = jnp.float32
    keys_all = jnp.repeat(key_soft.reshape(TOKENS, KV_HEADS, HEAD_DIM), HEAD_DEV, axis=1).astype(float_type)
    values_all = jnp.repeat(value_soft.reshape(TOKENS, KV_HEADS, HEAD_DIM), HEAD_DEV, axis=1).astype(float_type)
    key_pos = jnp.arange(TOKENS, dtype=jnp.int32)
    query_blocks = query_soft.reshape(N_CTX, TOK_DEV, HEADS, HEAD_DIM)
    scale = 1.0 / math.sqrt(HEAD_DIM)

    def attend(block_args):
        block_query, block_index = block_args
        query_pos = block_index * TOK_DEV + jnp.arange(TOK_DEV, dtype=jnp.int32)
        scores = jnp.einsum('qhd,khd->hqk', block_query.astype(float_type), keys_all) * scale
        allowed = key_pos[None, None, :] <= query_pos[None, :, None]
        row_max = lax.optimization_barrier(jnp.max(jnp.where(allowed, scores, -1e+30), axis=-1, keepdims=True))
        exponent = jnp.where(allowed, jnp.exp(scores - row_max), 0.0)
        row_sum = lax.optimization_barrier(jnp.sum(exponent, axis=-1))
        weights = rounded(exponent)
        attended_block = jnp.einsum('hqk,khd->qhd', weights, values_all) / jnp.transpose(row_sum)[:, :, None]
        return attended_block.astype(jnp.bfloat16)
    attended = lax.map(attend, (query_blocks, jnp.arange(N_CTX, dtype=jnp.int32)))
    attended = attended.reshape(TOKENS, HEADS * HEAD_DIM)
    branch = jnp.dot(attended, out_weight, preferred_element_type=jnp.float32)
    normed = rms_rows(hidden_in.astype(float_type) + branch).astype(jnp.bfloat16)
    lin_query = rounded(jnp.dot(normed, query_weight, preferred_element_type=jnp.float32)).reshape(N_CTX, TOK_DEV, HEADS, HEAD_DIM)
    lin_key = rounded(jnp.dot(normed, key_weight, preferred_element_type=jnp.float32)).reshape(N_CTX, TOK_DEV, HEADS, HEAD_DIM)
    lin_value = rounded(jnp.dot(normed, value_weight, preferred_element_type=jnp.float32)).reshape(N_CTX, TOK_DEV, HEADS, HEAD_DIM)
    block_state = jnp.einsum('nthd,nthe->nhde', lin_key, lin_value)
    prefix = jnp.cumsum(block_state, axis=0)
    carried = jnp.concatenate([jnp.zeros_like(block_state[:1]), prefix[:-1]], axis=0)
    carried = rounded(carried)
    carried_part = jnp.einsum('nthd,nhde->nthe', lin_query, carried)
    local_scores = jnp.einsum('nthd,nshd->nhts', lin_query, lin_key)
    causal = jnp.arange(TOK_DEV, dtype=jnp.int32)[:, None] >= jnp.arange(TOK_DEV, dtype=jnp.int32)[None, :]
    local_scores = rounded(jnp.where(causal[None, None], local_scores, 0.0))
    mixed_rows = carried_part + jnp.einsum('nhts,nshe->nthe', local_scores, lin_value)
    return rms_rows(mixed_rows).astype(jnp.bfloat16).reshape(TOKENS, HEADS * HEAD_DIM)
```

```python
import functools
import math

import jax
import jax.numpy as jnp
from jax import lax
from jax.experimental import pallas as pl
from jax.experimental.pallas import tpu as pltpu
from jax.sharding import PartitionSpec as P

HEAD_DIM = 128
HEAD_DEV = 2
F32 = jnp.float32
BF16 = jnp.bfloat16
VMEM = pl.BlockSpec(memory_space=pltpu.VMEM)
SMEM = pl.BlockSpec(memory_space=pltpu.SMEM)
NT = (((1,), (1,)), ((), ()))
TN = (((0,), (0,)), ((), ()))
EXACT = lax.Precision.HIGHEST


def rms_rows(values):
    return values * lax.rsqrt(jnp.mean(values * values, axis=-1, keepdims=True) + 1e-06)


def attend_block(carry, key_rows, value_rows, key_start, query_pos, queries):
    run_max, run_sum, run_out = carry
    scores = jnp.einsum("qhd,kd->hqk", queries, key_rows, preferred_element_type=F32) * (
        1.0 / math.sqrt(HEAD_DIM)
    )
    key_pos = key_start + lax.iota(jnp.int32, key_rows.shape[0])
    allowed = key_pos[None, None, :] <= query_pos[None, :, None]
    fresh_max = jnp.maximum(run_max, jnp.max(jnp.where(allowed, scores, -1e30), axis=-1))
    weights = jnp.where(allowed, jnp.exp(scores - fresh_max[:, :, None]), 0.0)
    factor = jnp.exp(run_max - fresh_max)
    run_sum = run_sum * factor + jnp.sum(weights, axis=-1)
    run_out = run_out * factor[:, :, None] + jnp.einsum(
        "hqk,kd->hqd", weights.astype(BF16), value_rows, preferred_element_type=F32
    )
    return (fresh_max, run_sum, run_out)


def largest_divisor(whole, limit):
    best = 1
    for trial in range(1, min(whole, limit) + 1):
        if whole % trial == 0:
            best = trial
    return best


def general_body(
    hidden_in, query_soft, key_soft, value_soft, out_weight, query_weight, key_weight, value_weight
):
    row_count = hidden_in.shape[0]
    head_width = HEAD_DEV * HEAD_DIM
    position, length = lax.axis_index("ctx"), lax.axis_size("ctx")
    queries = query_soft.reshape(row_count, HEAD_DEV, HEAD_DIM)
    query_pos = position * row_count + lax.iota(jnp.int32, row_count)
    carry = (
        jnp.full((HEAD_DEV, row_count), -1e30, F32),
        jnp.zeros((HEAD_DEV, row_count), F32),
        jnp.zeros((HEAD_DEV, row_count, HEAD_DIM), F32),
    )
    span = row_count * largest_divisor(length, max(1, 2048 // row_count))
    keys = lax.all_gather(key_soft, "ctx", axis=0, tiled=True).reshape(-1, span, HEAD_DIM)
    values = lax.all_gather(value_soft, "ctx", axis=0, tiled=True).reshape(-1, span, HEAD_DIM)

    def step(carry_now, item):
        key_rows, value_rows, index = item
        result = lax.cond(
            index * span <= query_pos[-1],
            lambda inner: attend_block(
                inner, key_rows, value_rows, index * span, query_pos, queries
            ),
            lambda inner: inner,
            carry_now,
        )
        return (result, None)

    carry, _ = lax.scan(step, carry, (keys, values, jnp.arange(keys.shape[0], dtype=jnp.int32)))
    _, run_sum, run_out = carry
    attended = (run_out / run_sum[:, :, None]).astype(BF16)
    attended = jnp.transpose(attended, (1, 0, 2)).reshape(row_count, head_width)
    summed = lax.psum(
        jnp.dot(attended, out_weight, preferred_element_type=F32).astype(BF16), "head"
    ).astype(F32)
    normed = rms_rows(hidden_in.astype(F32) + summed).astype(BF16)
    lin_query, lin_key, lin_value = (
        jnp.dot(normed, weight, preferred_element_type=F32)
        .astype(BF16)
        .reshape(row_count, HEAD_DEV, HEAD_DIM)
        for weight in (query_weight, key_weight, value_weight)
    )
    block_state = jnp.einsum("thd,the->hde", lin_key, lin_value, preferred_element_type=F32)
    everything = lax.all_gather(block_state.astype(BF16), "ctx")

    def lap(k, before):
        return jnp.where(k < position, before + everything[k].astype(F32), before)

    carried = lax.fori_loop(0, length, lap, jnp.zeros_like(block_state)).astype(BF16)
    carried_part = jnp.einsum("thd,hde->the", lin_query, carried, preferred_element_type=F32)
    local_scores = jnp.einsum("thd,shd->hts", lin_query, lin_key, preferred_element_type=F32)
    causal = lax.iota(jnp.int32, row_count)[:, None] >= lax.iota(jnp.int32, row_count)[None, :]
    local_scores = jnp.where(causal[None], local_scores, 0.0).astype(BF16)
    mixed_rows = carried_part + jnp.einsum(
        "hts,she->the", local_scores, lin_value, preferred_element_type=F32
    )
    return rms_rows(mixed_rows).astype(BF16).reshape(row_count, head_width)


def causal_rows(shape, first_row):
    rows = lax.broadcasted_iota(jnp.int32, shape, 0) + first_row
    return lax.broadcasted_iota(jnp.int32, shape, 1) <= rows


def attend_kernel(place, query, pair, out):
    rows = query.shape[0]
    keys = pair[:, :HEAD_DIM]
    values = pair[:, HEAD_DIM:]
    allowed = causal_rows((rows, keys.shape[0]), place[0] * rows)
    for head in range(HEAD_DEV):
        columns = slice(head * HEAD_DIM, (head + 1) * HEAD_DIM)
        scores = lax.dot_general(query[:, columns], keys, NT, preferred_element_type=F32)
        scores = jnp.where(allowed, scores * (1.0 / math.sqrt(HEAD_DIM)), -1e30)
        weights = jnp.exp(scores - jnp.max(scores, axis=-1, keepdims=True))
        total = jnp.sum(weights, axis=-1, keepdims=True)
        summed = jnp.dot(weights.astype(BF16), values, preferred_element_type=F32)
        out[:, columns] = (summed / total).astype(BF16)


def fold_step(lhs, query_w, key_w, value_w, out_w, total):
    width = query_w.shape[1]

    @pl.when(pl.program_id(0) == 0)
    def _():
        total[...] = jnp.zeros_like(total)

    for index, weight in enumerate((query_w, key_w, value_w)):
        total[:, index * width : (index + 1) * width] += jnp.dot(
            lhs, weight[...], preferred_element_type=F32
        )
    total[:, 3 * width :] += lax.dot_general(lhs, out_w[...], NT, preferred_element_type=F32)


def early_kernel(hidden, first, second, qw, kw, vw, ow, plain, squares, folded, total):
    lhs = jnp.concatenate([hidden[...], first[...], second[...]], axis=0)
    rows = hidden.shape[0]
    values = hidden[...].astype(F32)
    sums = jnp.sum(values * values, axis=-1, keepdims=True)

    @pl.when(pl.program_id(0) == 0)
    def _():
        squares[...] = jnp.zeros_like(squares)

    squares[...] += jnp.broadcast_to(sums, squares.shape)
    fold_step(lhs, qw, kw, vw, ow, total)

    @pl.when(pl.program_id(0) == pl.num_programs(0) - 1)
    def _():
        plain[...] = total[:rows, :]
        folded[...] = total[rows:, :].astype(BF16)


def late_kernel(first, second, qw, kw, vw, ow, folded, total):
    fold_step(jnp.concatenate([first[...], second[...]], axis=0), qw, kw, vw, ow, total)

    @pl.when(pl.program_id(0) == pl.num_programs(0) - 1)
    def _():
        folded[...] = total[...].astype(BF16)


def fold_specs(lhs_rows, width, depth):
    return [pl.BlockSpec((rows, depth), lambda k: (0, k)) for rows in lhs_rows] + [
        pl.BlockSpec((depth, width), lambda k: (k, 0)) for _ in range(3)
    ] + [pl.BlockSpec((width, depth), lambda k: (0, k))]


def project_kernel(place, plain, a0, a1, a2, a3, *refs):
    blocks, (raw, part, table) = refs[:16], refs[16:]
    count = 8
    slice_rows = a0.shape[1] // count
    width = a0.shape[1]
    for stage in range(2):
        for step in range(count):
            block = blocks[stage * count + step]
            start = pl.multiple_of((place[0] ^ step) * slice_rows, slice_rows)
            for half in range(2):
                table[pl.ds((stage * 2 + half) * width + start, slice_rows), :] = block[
                    half * slice_rows : (half + 1) * slice_rows, :
                ]
    total = plain[:, : 3 * width]
    cross = 2.0 * plain[:, 3 * width :]
    for index, attended in enumerate((a0, a1, a2, a3)):
        product = jnp.dot(
            attended[...], table[index * width : (index + 1) * width, :],
            preferred_element_type=F32,
        )
        total += product[:, : 3 * width]
        cross += product[:, 3 * width :]
    raw[...] = total
    terms = a0[...].astype(F32) * cross
    part[...] = lax.dot_general(
        jnp.ones((8, width), F32), terms, NT, preferred_element_type=F32, precision=EXACT
    )


def state_kernel(model, raw, squares, p0, p1, p2, p3, packed, states):
    parts = p0[...] + p1[...] + p2[...] + p3[...]
    pick = jnp.where(lax.broadcasted_iota(jnp.int32, (8, HEAD_DIM), 0) == 0, 1.0, 0.0)
    column = lax.dot_general(parts, pick, TN, preferred_element_type=F32, precision=EXACT)
    mean = jnp.maximum(squares[...] + column, 0.0) * (1.0 / model)
    scale = lax.rsqrt(mean + 1e-06)
    for index in range(raw.shape[1] // HEAD_DIM):
        columns = slice(index * HEAD_DIM, (index + 1) * HEAD_DIM)
        packed[:, columns] = (raw[:, columns] * scale).astype(BF16)
    width = HEAD_DEV * HEAD_DIM
    for head in range(HEAD_DEV):
        start = width + head * HEAD_DIM
        states[head * HEAD_DIM : (head + 1) * HEAD_DIM, :] = lax.dot_general(
            packed[:, start : start + HEAD_DIM],
            packed[:, start + width : start + width + HEAD_DIM],
            TN,
            preferred_element_type=F32,
        ).astype(BF16)


def final_kernel(place, packed, states, out, carried):
    rows = packed.shape[0]
    width = HEAD_DEV * HEAD_DIM
    carried[...] = jnp.zeros_like(carried)
    for block in range(states.shape[0] // width):

        @pl.when(block < place[0])
        def _():
            carried[...] += states[block * width : (block + 1) * width, :].astype(F32)

    causal = causal_rows((rows, rows), 0)
    for head in range(HEAD_DEV):
        columns = slice(head * HEAD_DIM, (head + 1) * HEAD_DIM)
        query = packed[:, columns]
        key = packed[:, width + head * HEAD_DIM : width + (head + 1) * HEAD_DIM]
        value = packed[:, 2 * width + head * HEAD_DIM : 2 * width + (head + 1) * HEAD_DIM]
        local = lax.dot_general(query, key, NT, preferred_element_type=F32)
        local = jnp.where(causal, local, 0.0).astype(BF16)
        mixed = jnp.dot(query, carried[columns, :].astype(BF16), preferred_element_type=F32)
        mixed += jnp.dot(local, value, preferred_element_type=F32)
        out[:, columns] = rms_rows(mixed).astype(BF16)


def swap(x, axis, bit):
    return lax.ppermute(x, axis, [(i, i ^ bit) for i in range(lax.axis_size(axis))])


def spread(block):
    far = [block, None, swap(block, "ctx", 2), None, swap(block, "ctx", 4), None, swap(block, "ctx", 6), None]
    for index in (0, 2, 4, 6):
        far[index + 1] = swap(far[index], "ctx", 1)
    return far


def folded_body(
    hidden_in, query_soft, key_soft, value_soft, out_weight, query_weight, key_weight, value_weight
):
    rows, model = hidden_in.shape
    width = HEAD_DEV * HEAD_DIM
    ring = lax.axis_size("ctx")
    slice_rows = width // ring
    depth = 512
    position = lax.axis_index("ctx")
    place = position.astype(jnp.int32).reshape(1)

    s0 = lax.dynamic_slice(out_weight, (position * slice_rows, 0), (slice_rows, model))
    s2 = swap(s0, "head", 2)
    s1 = swap(s0, "head", 1)
    s3 = swap(s2, "head", 1)

    pair = lax.all_gather(
        jnp.concatenate([key_soft, value_soft], axis=1), "ctx", axis=0, tiled=True
    )
    a0 = pl.pallas_call(
        attend_kernel,
        out_shape=jax.ShapeDtypeStruct((rows, width), BF16),
        in_specs=[SMEM, VMEM, VMEM],
        out_specs=VMEM,
        name="attend",
    )(place, query_soft, pair)
    a1, a2, a3 = (swap(a0, "head", bit) for bit in (1, 2, 3))

    weights = (query_weight, key_weight, value_weight, out_weight)
    steps = model // depth
    plain, squares, early = pl.pallas_call(
        early_kernel,
        grid=(steps,),
        out_shape=(
            jax.ShapeDtypeStruct((rows, 4 * width), F32),
            jax.ShapeDtypeStruct((rows, HEAD_DIM), F32),
            jax.ShapeDtypeStruct((2 * slice_rows, 4 * width), BF16),
        ),
        in_specs=fold_specs((rows, slice_rows, slice_rows), width, depth),
        out_specs=(
            pl.BlockSpec((rows, 4 * width), lambda k: (0, 0)),
            pl.BlockSpec((rows, HEAD_DIM), lambda k: (0, 0)),
            pl.BlockSpec((2 * slice_rows, 4 * width), lambda k: (0, 0)),
        ),
        scratch_shapes=[pltpu.VMEM((rows + 2 * slice_rows, 4 * width), F32)],
        name="fold_early",
    )(hidden_in, s0, s1, *weights)
    early_blocks = spread(early)
    late = pl.pallas_call(
        late_kernel,
        grid=(steps,),
        out_shape=jax.ShapeDtypeStruct((2 * slice_rows, 4 * width), BF16),
        in_specs=fold_specs((slice_rows, slice_rows), width, depth),
        out_specs=pl.BlockSpec((2 * slice_rows, 4 * width), lambda k: (0, 0)),
        scratch_shapes=[pltpu.VMEM((2 * slice_rows, 4 * width), F32)],
        name="fold_late",
    )(s2, s3, *weights)
    late_blocks = spread(late)

    raw, part = pl.pallas_call(
        project_kernel,
        out_shape=(
            jax.ShapeDtypeStruct((rows, 3 * width), F32),
            jax.ShapeDtypeStruct((8, rows), F32),
        ),
        in_specs=[SMEM] + [VMEM] * 21,
        out_specs=(VMEM, VMEM),
        scratch_shapes=[pltpu.VMEM((4 * width, 4 * width), BF16)],
        name="project",
    )(place, plain, a0, a1, a2, a3, *early_blocks, *late_blocks)
    parts = [part] + [swap(part, "head", bit) for bit in (1, 2, 3)]
    packed, states = pl.pallas_call(
        functools.partial(state_kernel, model),
        out_shape=(
            jax.ShapeDtypeStruct((rows, 3 * width), BF16),
            jax.ShapeDtypeStruct((width, HEAD_DIM), BF16),
        ),
        in_specs=[VMEM] * 6,
        out_specs=(VMEM, VMEM),
        name="state",
    )(raw, squares, *parts)
    everything = lax.all_gather(states, "ctx", axis=0, tiled=True)
    return pl.pallas_call(
        final_kernel,
        out_shape=jax.ShapeDtypeStruct((rows, width), BF16),
        in_specs=[SMEM, VMEM, VMEM],
        out_specs=VMEM,
        scratch_shapes=[pltpu.VMEM((width, HEAD_DIM), F32)],
        name="final",
    )(place, packed, everything)


def solution(mesh):
    small = mesh.shape["ctx"] == 8 and mesh.shape["head"] == 4
    return jax.shard_map(
        folded_body if small else general_body,
        mesh=mesh,
        in_specs=(
            P("ctx", None),
            P("ctx", "head"),
            P("ctx", "head"),
            P("ctx", "head"),
            P("head", None),
            P(None, "head"),
            P(None, "head"),
            P(None, "head"),
        ),
        out_specs=P("ctx", "head"),
        check_vma=False,
    )
```

```python
import functools
import math

import jax
import jax.numpy as jnp
from jax import lax
from jax.experimental import pallas as pl
from jax.experimental.pallas import tpu as pltpu
from jax.sharding import PartitionSpec as P


HEAD_DIM = 128
HEAD_DEV = 2
F32 = jnp.float32
BF16 = jnp.bfloat16
VMEM = pl.BlockSpec(memory_space=pltpu.VMEM)
SMEM = pl.BlockSpec(memory_space=pltpu.SMEM)
FAR = pl.BlockSpec(memory_space=pltpu.HBM)
NT = (((1,), (1,)), ((), ()))
TN = (((0,), (0,)), ((), ()))
EXACT = lax.Precision.HIGHEST
MIB = 1 << 20


def limit(mib):
    return pltpu.CompilerParams(vmem_limit_bytes=mib * MIB)


def rms_rows(values):
    return values * lax.rsqrt(jnp.mean(values * values, axis=-1, keepdims=True) + 1e-06)


def attend_block(carry, key_rows, value_rows, key_start, query_pos, queries):
    run_max, run_sum, run_out = carry
    scores = jnp.einsum("qhd,kd->hqk", queries, key_rows, preferred_element_type=F32) * (
        1.0 / math.sqrt(HEAD_DIM)
    )
    key_pos = key_start + lax.iota(jnp.int32, key_rows.shape[0])
    allowed = key_pos[None, None, :] <= query_pos[None, :, None]
    fresh_max = jnp.maximum(run_max, jnp.max(jnp.where(allowed, scores, -1e30), axis=-1))
    weights = jnp.where(allowed, jnp.exp(scores - fresh_max[:, :, None]), 0.0)
    factor = jnp.exp(run_max - fresh_max)
    run_sum = run_sum * factor + jnp.sum(weights, axis=-1)
    run_out = run_out * factor[:, :, None] + jnp.einsum(
        "hqk,kd->hqd", weights.astype(BF16), value_rows, preferred_element_type=F32
    )
    return (fresh_max, run_sum, run_out)


def largest_divisor(whole, limit):
    best = 1
    for trial in range(1, min(whole, limit) + 1):
        if whole % trial == 0:
            best = trial
    return best


def general_body(
    hidden_in, query_soft, key_soft, value_soft, out_weight, query_weight, key_weight, value_weight
):
    row_count = hidden_in.shape[0]
    head_width = HEAD_DEV * HEAD_DIM
    position, length = lax.axis_index("ctx"), lax.axis_size("ctx")
    queries = query_soft.reshape(row_count, HEAD_DEV, HEAD_DIM)
    query_pos = position * row_count + lax.iota(jnp.int32, row_count)
    carry = (
        jnp.full((HEAD_DEV, row_count), -1e30, F32),
        jnp.zeros((HEAD_DEV, row_count), F32),
        jnp.zeros((HEAD_DEV, row_count, HEAD_DIM), F32),
    )
    span = row_count * largest_divisor(length, max(1, 2048 // row_count))
    keys = lax.all_gather(key_soft, "ctx", axis=0, tiled=True).reshape(-1, span, HEAD_DIM)
    values = lax.all_gather(value_soft, "ctx", axis=0, tiled=True).reshape(-1, span, HEAD_DIM)

    def step(carry_now, item):
        key_rows, value_rows, index = item
        result = lax.cond(
            index * span <= query_pos[-1],
            lambda inner: attend_block(
                inner, key_rows, value_rows, index * span, query_pos, queries
            ),
            lambda inner: inner,
            carry_now,
        )
        return (result, None)

    carry, _ = lax.scan(step, carry, (keys, values, jnp.arange(keys.shape[0], dtype=jnp.int32)))
    _, run_sum, run_out = carry
    attended = (run_out / run_sum[:, :, None]).astype(BF16)
    attended = jnp.transpose(attended, (1, 0, 2)).reshape(row_count, head_width)
    summed = lax.psum(
        jnp.dot(attended, out_weight, preferred_element_type=F32).astype(BF16), "head"
    ).astype(F32)
    normed = rms_rows(hidden_in.astype(F32) + summed).astype(BF16)
    lin_query, lin_key, lin_value = (
        jnp.dot(normed, weight, preferred_element_type=F32)
        .astype(BF16)
        .reshape(row_count, HEAD_DEV, HEAD_DIM)
        for weight in (query_weight, key_weight, value_weight)
    )
    block_state = jnp.einsum("thd,the->hde", lin_key, lin_value, preferred_element_type=F32)
    everything = lax.all_gather(block_state.astype(BF16), "ctx")

    def lap(k, before):
        return jnp.where(k < position, before + everything[k].astype(F32), before)

    carried = lax.fori_loop(0, length, lap, jnp.zeros_like(block_state)).astype(BF16)
    carried_part = jnp.einsum("thd,hde->the", lin_query, carried, preferred_element_type=F32)
    local_scores = jnp.einsum("thd,shd->hts", lin_query, lin_key, preferred_element_type=F32)
    causal = lax.iota(jnp.int32, row_count)[:, None] >= lax.iota(jnp.int32, row_count)[None, :]
    local_scores = jnp.where(causal[None], local_scores, 0.0).astype(BF16)
    mixed_rows = carried_part + jnp.einsum(
        "hts,she->the", local_scores, lin_value, preferred_element_type=F32
    )
    return rms_rows(mixed_rows).astype(BF16).reshape(row_count, head_width)


def causal_rows(shape, first_row):
    rows = lax.broadcasted_iota(jnp.int32, shape, 0) + first_row
    return lax.broadcasted_iota(jnp.int32, shape, 1) <= rows


def attend_kernel(place, query, *refs):
    blocks, out = refs[:-1], refs[-1]
    rows = query.shape[0]
    own = place[0]
    causal = causal_rows((rows, rows), 0)
    for head in range(HEAD_DEV):
        columns = slice(head * HEAD_DIM, (head + 1) * HEAD_DIM)
        scores = []
        for step, block in enumerate(blocks):
            allowed = causal if step == 0 else (own ^ step) < own
            product = lax.dot_general(
                query[:, columns], block[:, :HEAD_DIM], NT, preferred_element_type=F32
            )
            scores.append(jnp.where(allowed, product * (1.0 / math.sqrt(HEAD_DIM)), -1e30))
        peak = functools.reduce(jnp.maximum, scores)
        peak = jnp.max(peak, axis=-1, keepdims=True)
        sums, summed = 0.0, 0.0
        for step, block in enumerate(blocks):
            weights = jnp.exp(scores[step] - peak)
            sums += weights
            summed += jnp.dot(
                weights.astype(BF16), block[:, HEAD_DIM:], preferred_element_type=F32
            )
        total = jnp.sum(sums, axis=-1, keepdims=True)
        out[:, columns] = (summed / total).astype(BF16)


def stage_kernel(place, out_w, key, value, query, piece, pair, query_here, sems):
    count = piece.shape[0]
    start = pl.multiple_of(place[0] * count, count)
    copies = [
        pltpu.make_async_copy(source, target, sems.at[index])
        for index, (source, target) in enumerate(
            (
                (out_w.at[pl.ds(start, count), :], piece),
                (key, pair.at[:, :HEAD_DIM]),
                (value, pair.at[:, HEAD_DIM:]),
                (query, query_here),
            )
        )
    ]
    for copy in copies:
        copy.start()
    for copy in copies:
        copy.wait()


def plain_kernel(hidden, qw, kw, vw, ow, plain, cross, squares, qv, kv, vv, ov, sems):
    width = qw.shape[1]
    pairs = ((qw, qv), (kw, kv), (vw, vv), (ow, ov))
    copies = [
        pltpu.make_async_copy(source, target, sems.at[index])
        for index, (source, target) in enumerate(pairs)
    ]
    for copy in copies:
        copy.start()
    values = hidden[...].astype(F32)
    sums = jnp.sum(values * values, axis=-1, keepdims=True)
    squares[...] = jnp.broadcast_to(sums, squares.shape)
    for index, weight in enumerate((qv, kv, vv)):
        copies[index].wait()
        plain[:, index * width : (index + 1) * width] = jnp.dot(
            hidden[...], weight[...], preferred_element_type=F32
        )
    copies[3].wait()
    cross[...] = lax.dot_general(hidden[...], ov[...], NT, preferred_element_type=F32)


def join(blocks, lhs):
    count = blocks[0].shape[0]
    for index, block in enumerate(blocks):
        lhs[index * count : (index + 1) * count, :] = block[...]


def fold_cross_kernel(*refs):
    blocks, (out_w, folded, lhs) = refs[:-3], refs[-3:]
    join(blocks, lhs)
    folded[...] = lax.dot_general(
        lhs[...], out_w[...], NT, preferred_element_type=F32
    ).astype(BF16)


def fold_main_kernel(*refs):
    blocks, (*weights, folded, lhs) = refs[:-5], refs[-5:]
    join(blocks, lhs)
    width = weights[0].shape[1]
    for index, weight in enumerate(weights):
        folded[:, index * width : (index + 1) * width] = jnp.dot(
            lhs[...], weight[...], preferred_element_type=F32
        ).astype(BF16)


def fill(table, place, blocks, slice_rows):
    for stage in range(len(blocks) // 8):
        for step in range(8):
            block = blocks[stage * 8 + step]
            start = pl.multiple_of((place[0] ^ step) * slice_rows, slice_rows)
            parts = block.shape[0] // slice_rows
            for part in range(parts):
                base = (stage * parts + part) * 8 * slice_rows
                table[pl.ds(base + start, slice_rows), :] = block[
                    part * slice_rows : (part + 1) * slice_rows, :
                ]


def apply_table(total, table, attended):
    width = attended[0].shape[1]
    for index, rows in enumerate(attended):
        total += jnp.dot(
            rows[...], table[index * width : (index + 1) * width, :],
            preferred_element_type=F32,
        )
    return total


def cross_kernel(place, cross, a0, a1, a2, a3, *refs):
    blocks, (part, table) = refs[:-2], refs[-2:]
    fill(table, place, blocks, a0.shape[1] // 8)
    total = apply_table(2.0 * cross[...], table, (a0, a1, a2, a3))
    terms = a0[...].astype(F32) * total
    part[...] = lax.dot_general(
        jnp.ones((8, terms.shape[1]), F32), terms, NT,
        preferred_element_type=F32, precision=EXACT,
    )


def project_kernel(place, plain, a0, a1, a2, a3, *refs):
    blocks, (raw, table) = refs[:-2], refs[-2:]
    fill(table, place, blocks, a0.shape[1] // 8)
    raw[...] = apply_table(plain[...], table, (a0, a1, a2, a3))


def state_kernel(model, raw, squares, p0, p1, p2, p3, packed, states):
    parts = p0[...] + p1[...] + p2[...] + p3[...]
    pick = jnp.where(lax.broadcasted_iota(jnp.int32, (8, HEAD_DIM), 0) == 0, 1.0, 0.0)
    column = lax.dot_general(parts, pick, TN, preferred_element_type=F32, precision=EXACT)
    mean = jnp.maximum(squares[...] + column, 0.0) * (1.0 / model)
    scale = lax.rsqrt(mean + 1e-06)
    for index in range(raw.shape[1] // HEAD_DIM):
        columns = slice(index * HEAD_DIM, (index + 1) * HEAD_DIM)
        packed[:, columns] = (raw[:, columns] * scale).astype(BF16)
    width = HEAD_DEV * HEAD_DIM
    for head in range(HEAD_DEV):
        start = width + head * HEAD_DIM
        states[head * HEAD_DIM : (head + 1) * HEAD_DIM, :] = lax.dot_general(
            packed[:, start : start + HEAD_DIM],
            packed[:, start + width : start + width + HEAD_DIM],
            TN,
            preferred_element_type=F32,
        ).astype(BF16)


def final_kernel(place, packed, *refs):
    states, out = refs[:-1], refs[-1]
    rows = packed.shape[0]
    width = HEAD_DEV * HEAD_DIM
    own = place[0]
    carried = jnp.zeros((width, HEAD_DIM), F32)
    for step in range(1, len(states)):
        carried += jnp.where((own ^ step) < own, states[step][...].astype(F32), 0.0)
    carried = carried.astype(BF16)
    causal = causal_rows((rows, rows), 0)
    for head in range(HEAD_DEV):
        columns = slice(head * HEAD_DIM, (head + 1) * HEAD_DIM)
        query = packed[:, columns]
        key = packed[:, width + head * HEAD_DIM : width + (head + 1) * HEAD_DIM]
        value = packed[:, 2 * width + head * HEAD_DIM : 2 * width + (head + 1) * HEAD_DIM]
        local = lax.dot_general(query, key, NT, preferred_element_type=F32)
        local = jnp.where(causal, local, 0.0).astype(BF16)
        mixed = jnp.dot(query, carried[columns, :], preferred_element_type=F32)
        mixed += jnp.dot(local, value, preferred_element_type=F32)
        out[:, columns] = rms_rows(mixed).astype(BF16)


def swap(x, axis, bit):
    return lax.ppermute(x, axis, [(i, i ^ bit) for i in range(lax.axis_size(axis))])


def spread(block):
    far = {bit: swap(block, "ctx", bit) for bit in (6, 4, 2)}
    far[0] = block
    for bit in (0, 2, 4, 6):
        far[bit + 1] = swap(far[bit], "ctx", 1)
    return [far[bit] for bit in range(8)]


def like(shape, kind):
    return jax.ShapeDtypeStruct(shape, kind)


def call(kernel, mib, outs, args, scratch=(), spec=VMEM):
    return pl.pallas_call(
        kernel,
        out_shape=outs,
        in_specs=[SMEM if x.dtype == jnp.int32 else spec for x in args],
        out_specs=jax.tree.map(lambda _: VMEM, outs),
        scratch_shapes=list(scratch),
        compiler_params=limit(mib),
    )(*args)


def folded_body(
    hidden_in, query_soft, key_soft, value_soft, out_weight, query_weight, key_weight, value_weight
):
    rows, model = hidden_in.shape
    width = HEAD_DEV * HEAD_DIM
    slice_rows = width // lax.axis_size("ctx")
    place = lax.axis_index("ctx").astype(jnp.int32).reshape(1)

    s0, pair, query_here = call(
        stage_kernel,
        60,
        (like((slice_rows, model), BF16), like((rows, width), BF16), like((rows, width), BF16)),
        (place, out_weight, key_soft, value_soft, query_soft),
        [pltpu.SemaphoreType.DMA((4,))],
        FAR,
    )
    s2 = swap(s0, "head", 2)
    s1 = swap(s0, "head", 1)
    pairs = spread(pair)
    weight_shapes = [like((model, width), BF16)] * 3 + [like((width, model), BF16)]
    plain, cross, squares, *weights = pl.pallas_call(
        plain_kernel,
        out_shape=[
            like((rows, 3 * width), F32),
            like((rows, width), F32),
            like((rows, HEAD_DIM), F32),
        ] + weight_shapes,
        in_specs=[VMEM] + [FAR] * 4,
        out_specs=[VMEM] * 7,
        scratch_shapes=[pltpu.SemaphoreType.DMA((4,))],
        name="plain",
        compiler_params=limit(42),
    )(hidden_in, query_weight, key_weight, value_weight, out_weight)
    a0 = call(attend_kernel, 12, like((rows, width), BF16), (place, query_here, *pairs))
    a1, a2, a3 = (swap(a0, "head", bit) for bit in (1, 2, 3))
    s3 = swap(s2, "head", 1)
    attended = (a0, a1, a2, a3)

    def fold(kernel, blocks, part_weights, columns):
        count = len(blocks) * slice_rows
        product = call(
            kernel,
            14,
            like((count, columns), BF16),
            (*blocks, *part_weights),
            [pltpu.VMEM((count, model), BF16)],
        )
        return spread(product)

    early_main = fold(fold_main_kernel, (s0, s1), weights[:3], 3 * width)
    all_cross = fold(fold_cross_kernel, (s0, s1, s2, s3), weights[3:], width)
    late_main = fold(fold_main_kernel, (s2, s3), weights[:3], 3 * width)

    part = call(
        cross_kernel,
        8,
        like((8, rows), F32),
        (place, cross, *attended, *all_cross),
        [pltpu.VMEM((4 * width, width), BF16)],
    )
    parts = [part] + [swap(part, "head", bit) for bit in (1, 2, 3)]
    raw = call(
        project_kernel,
        12,
        like((rows, 3 * width), F32),
        (place, plain, *attended, *early_main, *late_main),
        [pltpu.VMEM((4 * width, 3 * width), BF16)],
    )
    packed, states = call(
        functools.partial(state_kernel, model),
        6,
        (like((rows, 3 * width), BF16), like((width, HEAD_DIM), BF16)),
        (raw, squares, *parts),
    )
    return call(final_kernel, 6, like((rows, width), BF16), (place, packed, *spread(states)))


def fast_body(*args):
    return folded_body(*args)


def solution(mesh):
    small = mesh.shape["ctx"] == 8 and mesh.shape["head"] == 4
    return jax.shard_map(
        fast_body if small else general_body,
        mesh=mesh,
        in_specs=(
            P("ctx", None),
            P("ctx", "head"),
            P("ctx", "head"),
            P("ctx", "head"),
            P("head", None),
            P(None, "head"),
            P(None, "head"),
            P(None, "head"),
        ),
        out_specs=P("ctx", "head"),
        check_vma=False,
    )
```

```python
import functools
import math

import jax
import jax.numpy as jnp
from jax import lax
from jax.experimental import pallas as pl
from jax.experimental.pallas import tpu as pltpu
from jax.sharding import PartitionSpec as P


HEAD_DIM = 128
HEAD_DEV = 2
F32 = jnp.float32
BF16 = jnp.bfloat16
VMEM = pl.BlockSpec(memory_space=pltpu.VMEM)
SMEM = pl.BlockSpec(memory_space=pltpu.SMEM)
FAR = pl.BlockSpec(memory_space=pltpu.HBM)
NT = (((1,), (1,)), ((), ()))
TN = (((0,), (0,)), ((), ()))
EXACT = lax.Precision.HIGHEST
MIB = 1 << 20
SLICE, PAIR = 52, 8


def limit(mib):
    return pltpu.CompilerParams(vmem_limit_bytes=mib * MIB)


def rms_rows(values):
    return values * lax.rsqrt(jnp.mean(values * values, axis=-1, keepdims=True) + 1e-06)


def attend_block(carry, key_rows, value_rows, key_start, query_pos, queries):
    run_max, run_sum, run_out = carry
    scores = jnp.einsum("qhd,kd->hqk", queries, key_rows, preferred_element_type=F32) * (
        1.0 / math.sqrt(HEAD_DIM)
    )
    key_pos = key_start + lax.iota(jnp.int32, key_rows.shape[0])
    allowed = key_pos[None, None, :] <= query_pos[None, :, None]
    fresh_max = jnp.maximum(run_max, jnp.max(jnp.where(allowed, scores, -1e30), axis=-1))
    weights = jnp.where(allowed, jnp.exp(scores - fresh_max[:, :, None]), 0.0)
    factor = jnp.exp(run_max - fresh_max)
    run_sum = run_sum * factor + jnp.sum(weights, axis=-1)
    run_out = run_out * factor[:, :, None] + jnp.einsum(
        "hqk,kd->hqd", weights.astype(BF16), value_rows, preferred_element_type=F32
    )
    return (fresh_max, run_sum, run_out)


def largest_divisor(whole, limit):
    best = 1
    for trial in range(1, min(whole, limit) + 1):
        if whole % trial == 0:
            best = trial
    return best


def general_body(
    hidden_in, query_soft, key_soft, value_soft, out_weight, query_weight, key_weight, value_weight
):
    row_count = hidden_in.shape[0]
    head_width = HEAD_DEV * HEAD_DIM
    position, length = lax.axis_index("ctx"), lax.axis_size("ctx")
    queries = query_soft.reshape(row_count, HEAD_DEV, HEAD_DIM)
    query_pos = position * row_count + lax.iota(jnp.int32, row_count)
    carry = (
        jnp.full((HEAD_DEV, row_count), -1e30, F32),
        jnp.zeros((HEAD_DEV, row_count), F32),
        jnp.zeros((HEAD_DEV, row_count, HEAD_DIM), F32),
    )
    span = row_count * largest_divisor(length, max(1, 2048 // row_count))
    keys = lax.all_gather(key_soft, "ctx", axis=0, tiled=True).reshape(-1, span, HEAD_DIM)
    values = lax.all_gather(value_soft, "ctx", axis=0, tiled=True).reshape(-1, span, HEAD_DIM)

    def step(carry_now, item):
        key_rows, value_rows, index = item
        result = lax.cond(
            index * span <= query_pos[-1],
            lambda inner: attend_block(
                inner, key_rows, value_rows, index * span, query_pos, queries
            ),
            lambda inner: inner,
            carry_now,
        )
        return (result, None)

    carry, _ = lax.scan(step, carry, (keys, values, jnp.arange(keys.shape[0], dtype=jnp.int32)))
    _, run_sum, run_out = carry
    attended = (run_out / run_sum[:, :, None]).astype(BF16)
    attended = jnp.transpose(attended, (1, 0, 2)).reshape(row_count, head_width)
    summed = lax.psum(
        jnp.dot(attended, out_weight, preferred_element_type=F32).astype(BF16), "head"
    ).astype(F32)
    normed = rms_rows(hidden_in.astype(F32) + summed).astype(BF16)
    lin_query, lin_key, lin_value = (
        jnp.dot(normed, weight, preferred_element_type=F32)
        .astype(BF16)
        .reshape(row_count, HEAD_DEV, HEAD_DIM)
        for weight in (query_weight, key_weight, value_weight)
    )
    block_state = jnp.einsum("thd,the->hde", lin_key, lin_value, preferred_element_type=F32)
    everything = lax.all_gather(block_state.astype(BF16), "ctx")

    def lap(k, before):
        return jnp.where(k < position, before + everything[k].astype(F32), before)

    carried = lax.fori_loop(0, length, lap, jnp.zeros_like(block_state)).astype(BF16)
    carried_part = jnp.einsum("thd,hde->the", lin_query, carried, preferred_element_type=F32)
    local_scores = jnp.einsum("thd,shd->hts", lin_query, lin_key, preferred_element_type=F32)
    causal = lax.iota(jnp.int32, row_count)[:, None] >= lax.iota(jnp.int32, row_count)[None, :]
    local_scores = jnp.where(causal[None], local_scores, 0.0).astype(BF16)
    mixed_rows = carried_part + jnp.einsum(
        "hts,she->the", local_scores, lin_value, preferred_element_type=F32
    )
    return rms_rows(mixed_rows).astype(BF16).reshape(row_count, head_width)


def causal_rows(shape, first_row):
    rows = lax.broadcasted_iota(jnp.int32, shape, 0) + first_row
    return lax.broadcasted_iota(jnp.int32, shape, 1) <= rows


def attend_kernel(place, query, *refs):
    blocks, out = refs[:-1], refs[-1]
    rows = query.shape[0]
    own = place[0]
    causal = causal_rows((rows, rows), 0)
    for head in range(HEAD_DEV):
        columns = slice(head * HEAD_DIM, (head + 1) * HEAD_DIM)
        scores = []
        for step, block in enumerate(blocks):
            allowed = causal if step == 0 else (own ^ step) < own
            product = lax.dot_general(
                query[:, columns], block[:, :HEAD_DIM], NT, preferred_element_type=F32
            )
            scores.append(jnp.where(allowed, product * (1.0 / math.sqrt(HEAD_DIM)), -1e30))
        peak = functools.reduce(jnp.maximum, scores)
        peak = jnp.max(peak, axis=-1, keepdims=True)
        sums, summed = 0.0, 0.0
        for step, block in enumerate(blocks):
            weights = jnp.exp(scores[step] - peak)
            sums += weights
            summed += jnp.dot(
                weights.astype(BF16), block[:, HEAD_DIM:], preferred_element_type=F32
            )
        total = jnp.sum(sums, axis=-1, keepdims=True)
        out[:, columns] = (summed / total).astype(BF16)


def run_copies(pairs, sems):
    copies = [
        pltpu.make_async_copy(source, target, sems.at[index])
        for index, (source, target) in enumerate(pairs)
    ]
    for copy in copies:
        copy.start()
    for copy in copies:
        copy.wait()


def slice_kernel(place, out_w, piece, sems):
    count = piece.shape[0]
    start = pl.multiple_of(place[0] * count, count)
    run_copies([(out_w.at[pl.ds(start, count), :], piece)], sems)


def pair_kernel(key, value, pair, sems):
    run_copies(
        [(key, pair.at[:, :HEAD_DIM]), (value, pair.at[:, HEAD_DIM:])], sems
    )


def plain_kernel(hidden, qw, kw, vw, ow, plain, cross, squares, qv, kv, vv, ov, sems):
    width = qw.shape[1]
    pairs = ((qw, qv), (kw, kv), (vw, vv), (ow, ov))
    copies = [
        pltpu.make_async_copy(source, target, sems.at[index])
        for index, (source, target) in enumerate(pairs)
    ]
    copies[0].start()
    copies[1].start()
    values = hidden[...].astype(F32)
    sums = jnp.sum(values * values, axis=-1, keepdims=True)
    squares[...] = jnp.broadcast_to(sums, squares.shape)
    for index, weight in enumerate((qv, kv, vv)):
        copies[index].wait()
        if index < 2:
            copies[index + 2].start()
        plain[:, index * width : (index + 1) * width] = jnp.dot(
            hidden[...], weight[...], preferred_element_type=F32
        )
    copies[3].wait()
    cross[...] = lax.dot_general(hidden[...], ov[...], NT, preferred_element_type=F32)


def join(blocks, lhs):
    count = blocks[0].shape[0]
    for index, block in enumerate(blocks):
        lhs[index * count : (index + 1) * count, :] = block[...]


def fold_kernel(*refs):
    blocks, (*weights, out_w, folded, lhs) = refs[:-6], refs[-6:]
    join(blocks, lhs)
    width = out_w.shape[0]
    for index, weight in enumerate(weights):
        folded[:, index * width : (index + 1) * width] = jnp.dot(
            lhs[...], weight[...], preferred_element_type=F32
        ).astype(BF16)
    folded[:, 3 * width :] = lax.dot_general(
        lhs[...], out_w[...], NT, preferred_element_type=F32
    ).astype(BF16)


def fill(table, place, blocks, slice_rows, columns):
    done = 0
    for first in range(0, len(blocks), 8):
        parts = blocks[first].shape[0] // slice_rows
        for step in range(8):
            start = pl.multiple_of((place[0] ^ step) * slice_rows, slice_rows)
            for part in range(parts):
                base = (done + part) * 8 * slice_rows
                table[pl.ds(base + start, slice_rows), :] = blocks[first + step][
                    part * slice_rows : (part + 1) * slice_rows, columns
                ]
        done += parts


def apply_table(total, table, attended):
    width = attended[0].shape[1]
    for index, rows in enumerate(attended):
        total += jnp.dot(
            rows[...], table[index * width : (index + 1) * width, :],
            preferred_element_type=F32,
        )
    return total


def cross_kernel(place, cross, a0, a1, a2, a3, *refs):
    blocks, (part, table) = refs[:-2], refs[-2:]
    width = a0.shape[1]
    fill(table, place, blocks, width // 8, slice(3 * width, 4 * width))
    total = apply_table(2.0 * cross[...], table, (a0, a1, a2, a3))
    terms = a0[...].astype(F32) * total
    part[...] = lax.dot_general(
        jnp.ones((8, terms.shape[1]), F32), terms, NT,
        preferred_element_type=F32, precision=EXACT,
    )


def project_kernel(place, plain, a0, a1, a2, a3, *refs):
    blocks, (raw, table) = refs[:-2], refs[-2:]
    width = a0.shape[1]
    fill(table, place, blocks, width // 8, slice(0, 3 * width))
    raw[...] = apply_table(plain[...], table, (a0, a1, a2, a3))


def state_kernel(model, raw, squares, p0, p1, p2, p3, packed, states):
    parts = p0[...] + p1[...] + p2[...] + p3[...]
    pick = jnp.where(lax.broadcasted_iota(jnp.int32, (8, HEAD_DIM), 0) == 0, 1.0, 0.0)
    column = lax.dot_general(parts, pick, TN, preferred_element_type=F32, precision=EXACT)
    mean = jnp.maximum(squares[...] + column, 0.0) * (1.0 / model)
    scale = lax.rsqrt(mean + 1e-06)
    for index in range(raw.shape[1] // HEAD_DIM):
        columns = slice(index * HEAD_DIM, (index + 1) * HEAD_DIM)
        packed[:, columns] = (raw[:, columns] * scale).astype(BF16)
    width = HEAD_DEV * HEAD_DIM
    for head in range(HEAD_DEV):
        start = width + head * HEAD_DIM
        states[head * HEAD_DIM : (head + 1) * HEAD_DIM, :] = lax.dot_general(
            packed[:, start : start + HEAD_DIM],
            packed[:, start + width : start + width + HEAD_DIM],
            TN,
            preferred_element_type=F32,
        ).astype(BF16)


def local_kernel(packed, mixed):
    rows = packed.shape[0]
    width = HEAD_DEV * HEAD_DIM
    causal = causal_rows((rows, rows), 0)
    for head in range(HEAD_DEV):
        columns = slice(head * HEAD_DIM, (head + 1) * HEAD_DIM)
        key = packed[:, width + head * HEAD_DIM : width + (head + 1) * HEAD_DIM]
        value = packed[:, 2 * width + head * HEAD_DIM : 2 * width + (head + 1) * HEAD_DIM]
        local = lax.dot_general(packed[:, columns], key, NT, preferred_element_type=F32)
        local = jnp.where(causal, local, 0.0).astype(BF16)
        mixed[:, columns] = jnp.dot(local, value, preferred_element_type=F32)


def final_kernel(place, packed, mixed, *refs):
    states, out = refs[:-1], refs[-1]
    width = HEAD_DEV * HEAD_DIM
    own = place[0]
    carried = jnp.zeros((width, HEAD_DIM), F32)
    for step in range(1, len(states)):
        carried += jnp.where((own ^ step) < own, states[step][...].astype(F32), 0.0)
    carried = carried.astype(BF16)
    for head in range(HEAD_DEV):
        columns = slice(head * HEAD_DIM, (head + 1) * HEAD_DIM)
        total = mixed[:, columns] + jnp.dot(
            packed[:, columns], carried[columns, :], preferred_element_type=F32
        )
        out[:, columns] = rms_rows(total).astype(BF16)


def swap(x, axis, bit):
    return lax.ppermute(x, axis, [(i, i ^ bit) for i in range(lax.axis_size(axis))])


def spread(block):
    far = {bit: swap(block, "ctx", bit) for bit in (6, 4, 2)}
    far[0] = block
    for bit in (0, 2, 4, 6):
        far[bit + 1] = swap(far[bit], "ctx", 1)
    return [far[bit] for bit in range(8)]


def like(shape, kind):
    return jax.ShapeDtypeStruct(shape, kind)


def call(kernel, mib, outs, args, scratch=(), spec=VMEM):
    return pl.pallas_call(
        kernel,
        out_shape=outs,
        in_specs=[SMEM if x.dtype == jnp.int32 else spec for x in args],
        out_specs=jax.tree.map(lambda _: VMEM, outs),
        scratch_shapes=list(scratch),
        compiler_params=limit(mib),
    )(*args)


def folded_body(
    hidden_in, query_soft, key_soft, value_soft, out_weight, query_weight, key_weight, value_weight
):
    rows, model = hidden_in.shape
    width = HEAD_DEV * HEAD_DIM
    slice_rows = width // lax.axis_size("ctx")
    place = lax.axis_index("ctx").astype(jnp.int32).reshape(1)

    s0 = call(
        slice_kernel,
        SLICE,
        like((slice_rows, model), BF16),
        (place, out_weight),
        [pltpu.SemaphoreType.DMA((1,))],
        FAR,
    )
    s2 = swap(s0, "head", 2)
    pair = call(
        pair_kernel,
        PAIR,
        like((rows, width), BF16),
        (key_soft, value_soft),
        [pltpu.SemaphoreType.DMA((2,))],
        FAR,
    )
    s1 = swap(s0, "head", 1)
    pairs = spread(pair)
    weight_shapes = [like((model, width), BF16)] * 3 + [like((width, model), BF16)]
    plain, cross, squares, *weights = pl.pallas_call(
        plain_kernel,
        out_shape=[
            like((rows, 3 * width), F32),
            like((rows, width), F32),
            like((rows, HEAD_DIM), F32),
        ] + weight_shapes,
        in_specs=[VMEM] + [FAR] * 4,
        out_specs=[VMEM] * 7,
        scratch_shapes=[pltpu.SemaphoreType.DMA((4,))],
        name="plain",
        compiler_params=limit(42),
    )(hidden_in, query_weight, key_weight, value_weight, out_weight)
    a0 = call(attend_kernel, 12, like((rows, width), BF16), (place, query_soft, *pairs))
    a2 = swap(a0, "head", 2)
    a1 = swap(a0, "head", 1)
    a3 = swap(a2, "head", 1)
    s3 = swap(s2, "head", 1)
    attended = (a0, a1, a2, a3)

    def fold(blocks):
        count = len(blocks) * slice_rows
        product = call(
            fold_kernel,
            14,
            like((count, 4 * width), BF16),
            (*blocks, *weights),
            [pltpu.VMEM((count, model), BF16)],
        )
        return spread(product)

    folded = fold((s0, s1, s2)) + fold((s3,))

    part = call(
        cross_kernel,
        8,
        like((8, rows), F32),
        (place, cross, *attended, *folded),
        [pltpu.VMEM((4 * width, width), BF16)],
    )
    parts = [part] + [swap(part, "head", bit) for bit in (1, 2, 3)]
    raw = call(
        project_kernel,
        12,
        like((rows, 3 * width), F32),
        (place, plain, *attended, *folded),
        [pltpu.VMEM((4 * width, 3 * width), BF16)],
    )
    packed, states = call(
        functools.partial(state_kernel, model),
        6,
        (like((rows, 3 * width), BF16), like((width, HEAD_DIM), BF16)),
        (raw, squares, *parts),
    )
    mixed = call(local_kernel, 6, like((rows, width), F32), (packed,))
    return call(final_kernel, 6, like((rows, width), BF16), (place, packed, mixed, *spread(states)))


def fast_body(*args):
    return folded_body(*args)


def solution(mesh):
    small = mesh.shape["ctx"] == 8 and mesh.shape["head"] == 4
    return jax.shard_map(
        fast_body if small else general_body,
        mesh=mesh,
        in_specs=(
            P("ctx", None),
            P("ctx", "head"),
            P("ctx", "head"),
            P("ctx", "head"),
            P("head", None),
            P(None, "head"),
            P(None, "head"),
            P(None, "head"),
        ),
        out_specs=P("ctx", "head"),
        check_vma=False,
    )
```

```python
import functools
import math

import jax
import jax.numpy as jnp
from jax import lax
from jax.experimental import pallas as pl
from jax.experimental.pallas import tpu as pltpu
from jax.sharding import PartitionSpec as P


HEAD_DIM = 128
HEAD_DEV = 2
F32 = jnp.float32
BF16 = jnp.bfloat16
VMEM = pl.BlockSpec(memory_space=pltpu.VMEM)
SMEM = pl.BlockSpec(memory_space=pltpu.SMEM)
FAR = pl.BlockSpec(memory_space=pltpu.HBM)
NT = (((1,), (1,)), ((), ()))
TN = (((0,), (0,)), ((), ()))
EXACT = lax.Precision.HIGHEST
MIB = 1 << 20
COST = {"attend": 10**10}
PLAIN = 14
SLICE, PAIR = 52, 8


def limit(mib):
    return pltpu.CompilerParams(vmem_limit_bytes=mib * MIB)


def rms_rows(values):
    return values * lax.rsqrt(jnp.mean(values * values, axis=-1, keepdims=True) + 1e-06)


def attend_block(carry, key_rows, value_rows, key_start, query_pos, queries):
    run_max, run_sum, run_out = carry
    scores = jnp.einsum("qhd,kd->hqk", queries, key_rows, preferred_element_type=F32) * (
        1.0 / math.sqrt(HEAD_DIM)
    )
    key_pos = key_start + lax.iota(jnp.int32, key_rows.shape[0])
    allowed = key_pos[None, None, :] <= query_pos[None, :, None]
    fresh_max = jnp.maximum(run_max, jnp.max(jnp.where(allowed, scores, -1e30), axis=-1))
    weights = jnp.where(allowed, jnp.exp(scores - fresh_max[:, :, None]), 0.0)
    factor = jnp.exp(run_max - fresh_max)
    run_sum = run_sum * factor + jnp.sum(weights, axis=-1)
    run_out = run_out * factor[:, :, None] + jnp.einsum(
        "hqk,kd->hqd", weights.astype(BF16), value_rows, preferred_element_type=F32
    )
    return (fresh_max, run_sum, run_out)


def largest_divisor(whole, limit):
    best = 1
    for trial in range(1, min(whole, limit) + 1):
        if whole % trial == 0:
            best = trial
    return best


def general_body(
    hidden_in, query_soft, key_soft, value_soft, out_weight, query_weight, key_weight, value_weight
):
    row_count = hidden_in.shape[0]
    head_width = HEAD_DEV * HEAD_DIM
    position, length = lax.axis_index("ctx"), lax.axis_size("ctx")
    queries = query_soft.reshape(row_count, HEAD_DEV, HEAD_DIM)
    query_pos = position * row_count + lax.iota(jnp.int32, row_count)
    carry = (
        jnp.full((HEAD_DEV, row_count), -1e30, F32),
        jnp.zeros((HEAD_DEV, row_count), F32),
        jnp.zeros((HEAD_DEV, row_count, HEAD_DIM), F32),
    )
    span = row_count * largest_divisor(length, max(1, 2048 // row_count))
    keys = lax.all_gather(key_soft, "ctx", axis=0, tiled=True).reshape(-1, span, HEAD_DIM)
    values = lax.all_gather(value_soft, "ctx", axis=0, tiled=True).reshape(-1, span, HEAD_DIM)

    def step(carry_now, item):
        key_rows, value_rows, index = item
        result = lax.cond(
            index * span <= query_pos[-1],
            lambda inner: attend_block(
                inner, key_rows, value_rows, index * span, query_pos, queries
            ),
            lambda inner: inner,
            carry_now,
        )
        return (result, None)

    carry, _ = lax.scan(step, carry, (keys, values, jnp.arange(keys.shape[0], dtype=jnp.int32)))
    _, run_sum, run_out = carry
    attended = (run_out / run_sum[:, :, None]).astype(BF16)
    attended = jnp.transpose(attended, (1, 0, 2)).reshape(row_count, head_width)
    summed = lax.psum(
        jnp.dot(attended, out_weight, preferred_element_type=F32).astype(BF16), "head"
    ).astype(F32)
    normed = rms_rows(hidden_in.astype(F32) + summed).astype(BF16)
    lin_query, lin_key, lin_value = (
        jnp.dot(normed, weight, preferred_element_type=F32)
        .astype(BF16)
        .reshape(row_count, HEAD_DEV, HEAD_DIM)
        for weight in (query_weight, key_weight, value_weight)
    )
    block_state = jnp.einsum("thd,the->hde", lin_key, lin_value, preferred_element_type=F32)
    everything = lax.all_gather(block_state.astype(BF16), "ctx")

    def lap(k, before):
        return jnp.where(k < position, before + everything[k].astype(F32), before)

    carried = lax.fori_loop(0, length, lap, jnp.zeros_like(block_state)).astype(BF16)
    carried_part = jnp.einsum("thd,hde->the", lin_query, carried, preferred_element_type=F32)
    local_scores = jnp.einsum("thd,shd->hts", lin_query, lin_key, preferred_element_type=F32)
    causal = lax.iota(jnp.int32, row_count)[:, None] >= lax.iota(jnp.int32, row_count)[None, :]
    local_scores = jnp.where(causal[None], local_scores, 0.0).astype(BF16)
    mixed_rows = carried_part + jnp.einsum(
        "hts,she->the", local_scores, lin_value, preferred_element_type=F32
    )
    return rms_rows(mixed_rows).astype(BF16).reshape(row_count, head_width)


def causal_rows(shape, first_row):
    rows = lax.broadcasted_iota(jnp.int32, shape, 0) + first_row
    return lax.broadcasted_iota(jnp.int32, shape, 1) <= rows


def attend_kernel(place, query, *refs):
    blocks, out = refs[:-1], refs[-1]
    rows = query.shape[0]
    own = place[0]
    causal = causal_rows((rows, rows), 0)
    for head in range(HEAD_DEV):
        columns = slice(head * HEAD_DIM, (head + 1) * HEAD_DIM)
        scores = []
        for step, block in enumerate(blocks):
            allowed = causal if step == 0 else (own ^ step) < own
            product = lax.dot_general(
                query[:, columns], block[:, :HEAD_DIM], NT, preferred_element_type=F32
            )
            scores.append(jnp.where(allowed, product * (1.0 / math.sqrt(HEAD_DIM)), -1e30))
        peak = functools.reduce(jnp.maximum, scores)
        peak = jnp.max(peak, axis=-1, keepdims=True)
        sums, summed = 0.0, 0.0
        for step, block in enumerate(blocks):
            weights = jnp.exp(scores[step] - peak)
            sums += weights
            summed += jnp.dot(
                weights.astype(BF16), block[:, HEAD_DIM:], preferred_element_type=F32
            )
        total = jnp.sum(sums, axis=-1, keepdims=True)
        out[:, columns] = (summed / total).astype(BF16)


def run_copies(pairs, sems):
    copies = [
        pltpu.make_async_copy(source, target, sems.at[index])
        for index, (source, target) in enumerate(pairs)
    ]
    for copy in copies:
        copy.start()
    for copy in copies:
        copy.wait()


def slice_kernel(place, out_w, piece, sems):
    count = piece.shape[0]
    start = pl.multiple_of(place[0] * count, count)
    run_copies([(out_w.at[pl.ds(start, count), :], piece)], sems)


def pair_kernel(key, value, pair, sems):
    run_copies(
        [(key, pair.at[:, :HEAD_DIM]), (value, pair.at[:, HEAD_DIM:])], sems
    )


def plain_kernel(hidden, qw, kw, vw, ow, plain, cross, squares):
    width = qw.shape[1]
    values = hidden[...].astype(F32)
    sums = jnp.sum(values * values, axis=-1, keepdims=True)
    squares[...] = jnp.broadcast_to(sums, squares.shape)
    for index, weight in enumerate((qw, kw, vw)):
        plain[:, index * width : (index + 1) * width] = jnp.dot(
            hidden[...], weight[...], preferred_element_type=F32
        )
    cross[...] = lax.dot_general(hidden[...], ow[...], NT, preferred_element_type=F32)


def join(blocks, lhs):
    count = blocks[0].shape[0]
    for index, block in enumerate(blocks):
        lhs[index * count : (index + 1) * count, :] = block[...]


def fold_kernel(*refs):
    blocks, (*weights, out_w, folded, lhs) = refs[:-6], refs[-6:]
    join(blocks, lhs)
    width = out_w.shape[0]
    for index, weight in enumerate(weights):
        folded[:, index * width : (index + 1) * width] = jnp.dot(
            lhs[...], weight[...], preferred_element_type=F32
        ).astype(BF16)
    folded[:, 3 * width :] = lax.dot_general(
        lhs[...], out_w[...], NT, preferred_element_type=F32
    ).astype(BF16)


def fill(table, place, blocks, slice_rows, columns):
    done = 0
    for first in range(0, len(blocks), 8):
        parts = blocks[first].shape[0] // slice_rows
        for step in range(8):
            start = pl.multiple_of((place[0] ^ step) * slice_rows, slice_rows)
            for part in range(parts):
                base = (done + part) * 8 * slice_rows
                table[pl.ds(base + start, slice_rows), :] = blocks[first + step][
                    part * slice_rows : (part + 1) * slice_rows, columns
                ]
        done += parts


def apply_table(total, table, attended):
    width = attended[0].shape[1]
    for index, rows in enumerate(attended):
        total += jnp.dot(
            rows[...], table[index * width : (index + 1) * width, :],
            preferred_element_type=F32,
        )
    return total


def cross_kernel(place, cross, a0, a1, a2, a3, *refs):
    blocks, (part, table) = refs[:-2], refs[-2:]
    width = a0.shape[1]
    fill(table, place, blocks, width // 8, slice(3 * width, 4 * width))
    total = apply_table(2.0 * cross[...], table, (a0, a1, a2, a3))
    terms = a0[...].astype(F32) * total
    part[...] = lax.dot_general(
        jnp.ones((8, terms.shape[1]), F32), terms, NT,
        preferred_element_type=F32, precision=EXACT,
    )


def project_kernel(place, plain, a0, a1, a2, a3, *refs):
    blocks, (raw, table) = refs[:-2], refs[-2:]
    width = a0.shape[1]
    fill(table, place, blocks, width // 8, slice(0, 3 * width))
    raw[...] = apply_table(plain[...], table, (a0, a1, a2, a3))


def state_kernel(model, raw, squares, p0, p1, p2, p3, packed, states):
    parts = p0[...] + p1[...] + p2[...] + p3[...]
    pick = jnp.where(lax.broadcasted_iota(jnp.int32, (8, HEAD_DIM), 0) == 0, 1.0, 0.0)
    column = lax.dot_general(parts, pick, TN, preferred_element_type=F32, precision=EXACT)
    mean = jnp.maximum(squares[...] + column, 0.0) * (1.0 / model)
    scale = lax.rsqrt(mean + 1e-06)
    for index in range(raw.shape[1] // HEAD_DIM):
        columns = slice(index * HEAD_DIM, (index + 1) * HEAD_DIM)
        packed[:, columns] = (raw[:, columns] * scale).astype(BF16)
    width = HEAD_DEV * HEAD_DIM
    for head in range(HEAD_DEV):
        start = width + head * HEAD_DIM
        states[head * HEAD_DIM : (head + 1) * HEAD_DIM, :] = lax.dot_general(
            packed[:, start : start + HEAD_DIM],
            packed[:, start + width : start + width + HEAD_DIM],
            TN,
            preferred_element_type=F32,
        ).astype(BF16)


def local_kernel(packed, mixed):
    rows = packed.shape[0]
    width = HEAD_DEV * HEAD_DIM
    causal = causal_rows((rows, rows), 0)
    for head in range(HEAD_DEV):
        columns = slice(head * HEAD_DIM, (head + 1) * HEAD_DIM)
        key = packed[:, width + head * HEAD_DIM : width + (head + 1) * HEAD_DIM]
        value = packed[:, 2 * width + head * HEAD_DIM : 2 * width + (head + 1) * HEAD_DIM]
        local = lax.dot_general(packed[:, columns], key, NT, preferred_element_type=F32)
        local = jnp.where(causal, local, 0.0).astype(BF16)
        mixed[:, columns] = jnp.dot(local, value, preferred_element_type=F32)


def final_kernel(place, packed, mixed, *refs):
    states, out = refs[:-1], refs[-1]
    width = HEAD_DEV * HEAD_DIM
    own = place[0]
    carried = jnp.zeros((width, HEAD_DIM), F32)
    for step in range(1, len(states)):
        carried += jnp.where((own ^ step) < own, states[step][...].astype(F32), 0.0)
    carried = carried.astype(BF16)
    for head in range(HEAD_DEV):
        columns = slice(head * HEAD_DIM, (head + 1) * HEAD_DIM)
        total = mixed[:, columns] + jnp.dot(
            packed[:, columns], carried[columns, :], preferred_element_type=F32
        )
        out[:, columns] = rms_rows(total).astype(BF16)


def swap(x, axis, bit):
    return lax.ppermute(x, axis, [(i, i ^ bit) for i in range(lax.axis_size(axis))])


def spread(block):
    far = {bit: swap(block, "ctx", bit) for bit in (6, 4, 2)}
    far[0] = block
    for bit in (0, 2, 4, 6):
        far[bit + 1] = swap(far[bit], "ctx", 1)
    return [far[bit] for bit in range(8)]


def like(shape, kind):
    return jax.ShapeDtypeStruct(shape, kind)


def call(kernel, name, mib, outs, args, scratch=(), spec=VMEM):
    return pl.pallas_call(
        kernel,
        out_shape=outs,
        in_specs=[SMEM if x.dtype == jnp.int32 else spec for x in args],
        out_specs=jax.tree.map(lambda _: VMEM, outs),
        scratch_shapes=list(scratch),
        compiler_params=limit(mib),
        cost_estimate=pl.CostEstimate(flops=COST.get(name, 0), transcendentals=0, bytes_accessed=0),
    )(*args)


def folded_body(
    hidden_in, query_soft, key_soft, value_soft, out_weight, query_weight, key_weight, value_weight
):
    rows, model = hidden_in.shape
    width = HEAD_DEV * HEAD_DIM
    slice_rows = width // lax.axis_size("ctx")
    place = lax.axis_index("ctx").astype(jnp.int32).reshape(1)

    s0 = call(
        slice_kernel,
        "slice",
        SLICE,
        like((slice_rows, model), BF16),
        (place, out_weight),
        [pltpu.SemaphoreType.DMA((1,))],
        FAR,
    )
    s2 = swap(s0, "head", 2)
    pair = call(
        pair_kernel,
        "pair",
        PAIR,
        like((rows, width), BF16),
        (key_soft, value_soft),
        [pltpu.SemaphoreType.DMA((2,))],
        FAR,
    )
    s1 = swap(s0, "head", 1)
    pairs = spread(pair)
    weights = (query_weight, key_weight, value_weight, out_weight)
    plain, cross, squares = call(
        plain_kernel,
        "plain",
        PLAIN,
        (
            like((rows, 3 * width), F32),
            like((rows, width), F32),
            like((rows, HEAD_DIM), F32),
        ),
        (hidden_in, *weights),
    )
    a0 = call(
        attend_kernel, "attend", 12, like((rows, width), BF16), (place, query_soft, *pairs)
    )
    a2 = swap(a0, "head", 2)
    a1 = swap(a0, "head", 1)
    a3 = swap(a2, "head", 1)
    s3 = swap(s2, "head", 1)
    attended = (a0, a1, a2, a3)

    def fold(label, blocks):
        count = len(blocks) * slice_rows
        product = call(
            fold_kernel,
            "fold_" + label,
            14,
            like((count, 4 * width), BF16),
            (*blocks, *weights),
            [pltpu.VMEM((count, model), BF16)],
        )
        return spread(product)

    folded = fold("e", (s0, s1, s2)) + fold("l", (s3,))

    part = call(
        cross_kernel,
        "cross",
        8,
        like((8, rows), F32),
        (place, cross, *attended, *folded),
        [pltpu.VMEM((4 * width, width), BF16)],
    )
    parts = [part] + [swap(part, "head", bit) for bit in (1, 2, 3)]
    raw = call(
        project_kernel,
        "project",
        12,
        like((rows, 3 * width), F32),
        (place, plain, *attended, *folded),
        [pltpu.VMEM((4 * width, 3 * width), BF16)],
    )
    packed, states = call(
        functools.partial(state_kernel, model),
        "state",
        6,
        (like((rows, 3 * width), BF16), like((width, HEAD_DIM), BF16)),
        (raw, squares, *parts),
    )
    mixed = call(local_kernel, "local", 6, like((rows, width), F32), (packed,))
    return call(
        final_kernel,
        "final",
        6,
        like((rows, width), BF16),
        (place, packed, mixed, *spread(states)),
    )


def fast_body(*args):
    return folded_body(*args)


def solution(mesh):
    small = mesh.shape["ctx"] == 8 and mesh.shape["head"] == 4
    return jax.shard_map(
        fast_body if small else general_body,
        mesh=mesh,
        in_specs=(
            P("ctx", None),
            P("ctx", "head"),
            P("ctx", "head"),
            P("ctx", "head"),
            P("head", None),
            P(None, "head"),
            P(None, "head"),
            P(None, "head"),
        ),
        out_specs=P("ctx", "head"),
        check_vma=False,
    )
```
